32 devices in a mesh: ctx: 8 (over y, x, core), page: 4 (over z).
Axes of the slice: x: 2, y: 2, z: 4, core: 2. Of those that a mesh axis runs over, the one named last changes fastest.
Arguments:
- queries: bfloat16 [2048, 8192], P('ctx', 'page'), may hold values from -200 to 200
- keys: bfloat16 [2048, 512], P('ctx', 'page'), may hold values from -6 to 6
- values: bfloat16 [2048, 512], P('ctx', 'page'), may hold values from -6 to 6
- span_table: int32 [16], replicated, may hold values from 0 to 15, each once
- page_slots: int32 [16], replicated, may hold values from 0 to 15, each once
Outputs:
- attended: bfloat16 [2048, 8192], P('ctx', 'page')
- cache_pages: bfloat16 [16, 4, 2, 128, 128], P('ctx')
- cache_scales: float32 [16, 4, 2], P('ctx')
The draws below stay inside these ranges and needn't reach their ends.
Inputs may be any that keep to these rules, and one draw needn't show every extreme that they name: Stored span i (rows i * 128 to (i + 1) * 128 - 1) holds prompt positions span_table[i] * 128 onward; every value appears once. `page_slots`: every slot is named by exactly one page.
All inputs are finite; a program needn't handle non-finite values. Where the reference program divides by a largest or mean magnitude, that divisor is 1e-20 or more.
Results may differ from the reference program's by a relative error of at most 0.0055.
Values may be sent and summed in bfloat16 or wider, within the bound.
A program may use at most 64 MiB of HBM per device.

```python
import jax
import jax.numpy as jnp
from jax import lax

HQ = 64
KVH = 4
DH = 128
PAGE = 128
SPAN = 128
TOKENS = 2048
SLOTS = 16
N_CTX = 8


def common_draw(key):
    key_rows = jax.random.truncated_normal(jax.random.fold_in(key, 11), -6.0, 6.0, (TOKENS, KVH * DH), jnp.float32)
    query_rows = jax.random.truncated_normal(jax.random.fold_in(key, 12), -6.0, 6.0, (TOKENS, HQ * DH), jnp.float32)
    return (query_rows, key_rows)


def draw_queries(key, part):
    return common_draw(key)[0].astype(jnp.bfloat16)


def draw_keys(key, part):
    return common_draw(key)[1].astype(jnp.bfloat16)


def level_of(stream_key, shape, pieces, smallest, high):
    gain, own = 1.0, jax.random.fold_in(stream_key, 6)
    for dim, blocks in pieces:
        draws = jnp.exp(jax.random.uniform(jax.random.fold_in(own, dim), (blocks,), jnp.float32, smallest / len(pieces), high / len(pieces)))
        gain = gain * jnp.repeat(draws, shape[dim] // blocks).reshape([-1 if axis == dim else 1 for axis in range(len(shape))])
    return gain


def gaussian(rng, shape, scale, limit, shards=(), kind=jnp.bfloat16):
    level = level_of(rng, shape, shards, -0.22, 0.18) if shards else 1.0
    values = jax.random.normal(rng, shape, jnp.float32) * scale * level
    return jnp.minimum(jnp.maximum(values, -limit), limit).astype(kind)


def setup_inputs(seed: int = 0) -> dict:
    splits = jax.random.split(jax.random.key(seed), 6)
    return {
        "queries": draw_queries(jax.random.fold_in(splits[5], 71), 0),
        "keys": draw_keys(jax.random.fold_in(splits[5], 71), 0),
        "values": gaussian(splits[2], (TOKENS, KVH * DH), 1.0, 6.0, ((0, 8), (1, 4))),
        "span_table": jax.random.permutation(splits[3], 2 * N_CTX).astype(jnp.int32),
        "page_slots": jax.random.permutation(splits[4], SLOTS).astype(jnp.int32),
    }


def reference(queries, keys, values, span_table, page_slots):
    rows = jnp.arange(TOKENS, dtype=jnp.int32)
    pos = span_table[rows // SPAN] * SPAN + rows % SPAN
    group = HQ // KVH
    key_heads = keys.reshape(TOKENS, KVH, DH).astype(jnp.float32)
    value_heads = values.reshape(TOKENS, KVH, DH).astype(jnp.float32)
    scale = DH ** -0.5

    def block(index):
        start = (index * SPAN).astype(jnp.int32)
        query_block = lax.dynamic_slice_in_dim(queries, start, SPAN, 0)
        query_block = query_block.reshape(SPAN, KVH, group, DH).astype(jnp.float32)
        query_pos = lax.dynamic_slice_in_dim(pos, start, SPAN, 0)
        score = jnp.einsum('qhgd,khd->hgqk', query_block, key_heads) * scale
        keep = pos[None, :] <= query_pos[:, None]
        score = jnp.where(keep[None, None], score, -1e30)
        top = jnp.max(score, axis=-1, keepdims=True)
        weight = jnp.where(keep[None, None], jnp.exp(score - top), 0.0)
        total = jnp.sum(weight, axis=-1)
        weight_b = weight.astype(jnp.bfloat16).astype(jnp.float32)
        summed = jnp.einsum('hgqk,khd->qhgd', weight_b, value_heads)
        result = summed / jnp.transpose(total, (2, 0, 1))[..., None]
        return result.reshape(SPAN, HQ * DH).astype(jnp.bfloat16)

    attended = lax.map(block, jnp.arange(TOKENS // SPAN, dtype=jnp.int32)).reshape(TOKENS, HQ * DH)
    key_pages = keys.reshape(SLOTS, PAGE, KVH, DH).transpose(0, 2, 1, 3)
    value_pages = values.reshape(SLOTS, PAGE, KVH, DH).transpose(0, 2, 1, 3)
    stacked = jnp.stack([key_pages, value_pages], axis=2)
    page_of_slot = jnp.zeros((SLOTS,), jnp.int32).at[page_slots].set(jnp.arange(SLOTS, dtype=jnp.int32))
    raw = stacked[page_of_slot].astype(jnp.float32)
    cache_scales = jnp.max(jnp.abs(raw), axis=(3, 4)) + 1e-6
    cache_pages = (raw / cache_scales[..., None, None]).astype(jnp.bfloat16)
    return attended, cache_pages, cache_scales
```

```python
import functools
import math

import jax
import jax.numpy as jnp
from jax import lax
from jax.experimental import pallas as pl
from jax.experimental.pallas import tpu as pltpu
from jax.sharding import PartitionSpec as P

DH = 128
PAGE = 128
SPAN = 128
HIDE = -1e30
MESH = pl.DeviceIdType.MESH


def kernel(
    n, n_page, heads, table_ref, slots_ref, q_ref, k_ref, v_ref,
    out_ref, cache_ref, scales_ref,
    kbuf, vbuf, kmask, vone, acc, top, send, recv, own_sem, page_send, page_recv,
):
    chips = n // 2
    spans = k_ref.shape[0]
    wide = 2 * spans * SPAN
    per = math.gcd(heads, 4)
    groups = heads // per
    size = per * SPAN
    me = lax.axis_index("ctx")
    page = lax.axis_index("page")
    chip = me // 2
    core = me % 2
    sibling = 2 * chip + 1 - core
    rate = DH ** (-0.5) * math.log2(math.e)

    def ahead(d):
        return 2 * ((chip + d) % chips) + core

    def behind(d, c):
        return 2 * ((chip + chips - d) % chips) + c

    barrier = pltpu.get_barrier_semaphore()
    for d in range(1, chips):
        pl.semaphore_signal(barrier, inc=1, device_id={"ctx": ahead(d)}, device_id_type=MESH)
    pl.semaphore_signal(barrier, inc=1, device_id={"ctx": sibling}, device_id_type=MESH)
    for d in range(1, n_page):
        pl.semaphore_signal(
            barrier, inc=1, device_id={"page": (page + d) % n_page}, device_id_type=MESH
        )
    pl.semaphore_wait(barrier, chips + n_page - 1)

    def slot(buf, owner):
        return buf.at[pl.ds(owner * spans, spans)]

    def remote(src, buf, owner, index, j, target):
        return pltpu.make_async_remote_copy(
            src_ref=src,
            dst_ref=slot(buf, owner),
            send_sem=send.at[index, j],
            recv_sem=recv.at[index, j],
            device_id={"ctx": target},
            device_id_type=MESH,
        )

    pairs = ((k_ref, kbuf), (v_ref, vbuf))
    started = []
    local = []
    for d in range(1, chips):
        for j, (src, buf) in enumerate(pairs):
            copy = remote(src, buf, me, d, j, ahead(d))
            copy.start()
            started.append(copy)
    for j, (src, buf) in enumerate(pairs):
        copy = remote(src, buf, me, 0, j, sibling)
        copy.start()
        started.append(copy)
        copy = pltpu.make_async_copy(src, slot(buf, me), own_sem.at[j])
        copy.start()
        local.append(copy)

    rows_at = lax.broadcasted_iota(jnp.int32, (SPAN, SPAN), 0)
    cols_at = lax.broadcasted_iota(jnp.int32, (SPAN, SPAN), 1)
    eye = jnp.where(rows_at == cols_at, 1.0, 0.0).astype(jnp.bfloat16)
    vone[:, DH:] = jnp.ones((wide, DH), jnp.bfloat16)

    def chunk(d, first):
        owner = (chip + chips - d) % chips
        begin = owner * 2 * spans
        for t in range(2 * spans):
            place = pl.ds(t * SPAN, SPAN)
            piece = kbuf[begin + t]
            vone[place, :DH] = vbuf[begin + t]
            for i in range(spans):
                gap = (table_ref[me * spans + i] - table_ref[begin + t]) * SPAN
                kmask[i, place, :DH] = piece
                kmask[i, place, DH:] = jnp.where(rows_at - cols_at > gap, HIDE, 0.0).astype(
                    jnp.bfloat16
                )

        @pl.loop(0, groups)
        def _(g):
            for i in range(spans):
                lines = pl.ds(i * SPAN, SPAN)
                query = jnp.concatenate(
                    [
                        jnp.concatenate(
                            [
                                q_ref[lines, pl.ds(pl.multiple_of((g * per + h) * DH, DH), DH)],
                                eye,
                            ],
                            axis=1,
                        )
                        for h in range(per)
                    ],
                    axis=0,
                )
                score = lax.dot_general(
                    query, kmask[i], (((1,), (1,)), ((), ())), preferred_element_type=jnp.float32
                )
                high = jnp.broadcast_to(jnp.max(score, axis=1, keepdims=True), (size, DH))
                if not first:
                    old = top[g, i]
                    high = jnp.maximum(high, old)
                weight = jnp.concatenate(
                    [
                        jnp.exp2((score[:, t * SPAN : (t + 1) * SPAN] - high) * rate).astype(
                            jnp.bfloat16
                        )
                        for t in range(2 * spans)
                    ],
                    axis=1,
                )
                update = jnp.dot(weight, vone[...], preferred_element_type=jnp.float32)
                top[g, i] = high
                if first:
                    acc[g, i] = update
                else:
                    factor = jnp.exp2((old - high) * rate)
                    acc[g, i, :, :DH] = acc[g, i, :, :DH] * factor + update[:, :DH]
                    acc[g, i, :, DH:] = acc[g, i, :, DH:] * factor + update[:, DH:]

    for copy in local:
        copy.wait()
    for j, (src, buf) in enumerate(pairs):
        remote(src, buf, sibling, 0, j, sibling).wait_recv()
    chunk(0, True)

    for d in range(1, chips):
        for j, (src, buf) in enumerate(pairs):
            origin = behind(d, core)
            remote(src, buf, origin, d, j, sibling).wait_recv()
            copy = remote(slot(buf, origin), buf, origin, chips - 1 + d, j, sibling)
            copy.start()
            started.append(copy)
    for d in range(1, chips):
        for j, (src, buf) in enumerate(pairs):
            remote(src, buf, behind(d, 1 - core), chips - 1 + d, j, sibling).wait_recv()

    for s in range(spans):
        wanted = jnp.int32(0)
        for p in range(slots_ref.shape[0]):
            wanted = jnp.where(slots_ref[p] == me * spans + s, p, wanted)
        for j, buf in enumerate((kbuf, vbuf)):
            raw = buf[wanted].astype(jnp.float32)
            level = jnp.max(jnp.max(jnp.abs(raw), axis=0, keepdims=True), axis=1, keepdims=True)
            level = level + 1e-06
            cache_ref[page, s, j] = (raw / level).astype(jnp.bfloat16)
            scales_ref[page, s, j] = jnp.broadcast_to(level, (8, DH))

    def pages(index, target):
        return [
            pltpu.make_async_remote_copy(
                src_ref=ref.at[page],
                dst_ref=ref.at[page],
                send_sem=page_send.at[index, j],
                recv_sem=page_recv.at[index, j],
                device_id={"page": target},
                device_id_type=MESH,
            )
            for j, ref in enumerate((cache_ref, scales_ref))
        ]

    def arrived(index):
        origin = (page + n_page - index) % n_page
        for j, ref in enumerate((cache_ref, scales_ref)):
            pltpu.make_async_remote_copy(
                src_ref=ref.at[origin],
                dst_ref=ref.at[origin],
                send_sem=page_send.at[index, j],
                recv_sem=page_recv.at[index, j],
                device_id={"page": (page + index) % n_page},
                device_id_type=MESH,
            ).wait_recv()

    for d in range(1, chips):
        chunk(d, False)
        if d == 1:
            for index in range(1, n_page):
                for copy in pages(index, (page + index) % n_page):
                    copy.start()
                    started.append(copy)

    @pl.loop(0, groups)
    def _(g):
        for i in range(spans):
            for h in range(per):
                lines = pl.ds(h * SPAN, SPAN)
                out_ref[
                    pl.ds(i * SPAN, SPAN), pl.ds(pl.multiple_of((g * per + h) * DH, DH), DH)
                ] = (acc[g, i, lines, :DH] / acc[g, i, lines, DH:]).astype(jnp.bfloat16)

    for index in range(1, n_page):
        arrived(index)
    for copy in started:
        copy.wait_send()


def on_device(n, n_page, queries, keys, values, span_table, page_slots):
    rows = queries.shape[0]
    heads = queries.shape[1] // DH
    spans = rows // SPAN
    per = math.gcd(heads, 4)
    groups = heads // per
    chips = n // 2
    wide = 2 * rows
    vmem = pl.BlockSpec(memory_space=pltpu.VMEM)
    smem = pl.BlockSpec(memory_space=pltpu.SMEM)
    attended, cache, scales = pl.pallas_call(
        functools.partial(kernel, n, n_page, heads),
        out_shape=(
            jax.ShapeDtypeStruct((rows, heads * DH), jnp.bfloat16),
            jax.ShapeDtypeStruct((n_page, spans, 2, PAGE, DH), jnp.bfloat16),
            jax.ShapeDtypeStruct((n_page, spans, 2, 8, DH), jnp.float32),
        ),
        in_specs=[smem, smem, vmem, vmem, vmem],
        out_specs=(vmem, vmem, vmem),
        scratch_shapes=[
            pltpu.VMEM((n * spans, SPAN, DH), jnp.bfloat16),
            pltpu.VMEM((n * spans, SPAN, DH), jnp.bfloat16),
            pltpu.VMEM((spans, wide, 2 * DH), jnp.bfloat16),
            pltpu.VMEM((wide, 2 * DH), jnp.bfloat16),
            pltpu.VMEM((groups, spans, per * SPAN, 2 * DH), jnp.float32),
            pltpu.VMEM((groups, spans, per * SPAN, DH), jnp.float32),
            pltpu.SemaphoreType.DMA((n, 2)),
            pltpu.SemaphoreType.DMA((n, 2)),
            pltpu.SemaphoreType.DMA((2,)),
            pltpu.SemaphoreType.DMA((n_page, 2)),
            pltpu.SemaphoreType.DMA((n_page, 2)),
        ],
        compiler_params=pltpu.CompilerParams(
            collective_id=0, has_side_effects=True, vmem_limit_bytes=48 * 1024 * 1024
        ),
    )(
        span_table,
        page_slots,
        queries,
        keys.reshape(spans, SPAN, DH),
        values.reshape(spans, SPAN, DH),
    )
    cache = cache.transpose(1, 0, 2, 3, 4)
    scales = scales[:, :, :, 0, 0].transpose(1, 0, 2)
    return attended, cache, scales


def solution(mesh):
    placed = (P("ctx", "page"), P("ctx", "page"), P("ctx", "page"), P(), P())
    return jax.shard_map(
        functools.partial(on_device, mesh.shape["ctx"], mesh.shape["page"]),
        mesh=mesh,
        in_specs=placed,
        out_specs=(P("ctx", "page"), P("ctx", None, None, None, None), P("ctx", None, None)),
        check_vma=False,
    )
```

```python
import functools
import math

import jax
import jax.numpy as jnp
from jax import lax
from jax.experimental import pallas as pl
from jax.experimental.pallas import tpu as pltpu
from jax.sharding import PartitionSpec as P

DH = 128
PAGE = 128
SPAN = 128
HIDE = -1e30
MESH = pl.DeviceIdType.MESH


def kernel(
    n, n_page, heads, table_in, slots_in, q_in, k_ref, v_ref,
    out_ref, cache_ref, scales_ref,
    table_ref, slots_ref, q_ref,
    kbuf, vbuf, kmask, vone, acc, top, send, recv, own_sem, page_send, page_recv,
):
    chips = n // 2
    spans = k_ref.shape[0]
    wide = 2 * spans * SPAN
    per = math.gcd(heads, 4)
    groups = heads // per
    size = per * SPAN
    me = lax.axis_index("ctx")
    page = lax.axis_index("page")
    chip = me // 2
    core = me % 2
    sibling = 2 * chip + 1 - core
    rate = DH ** (-0.5) * math.log2(math.e)

    def ahead(d):
        return 2 * ((chip + d) % chips) + core

    def behind(d, c):
        return 2 * ((chip + chips - d) % chips) + c

    local = []

    def fetch(src, dst, j):
        copy = pltpu.make_async_copy(src, dst, own_sem.at[j])
        copy.start()
        local.append(copy)

    barrier = pltpu.get_barrier_semaphore()
    for d in range(1, chips):
        pl.semaphore_signal(barrier, inc=1, device_id={"ctx": ahead(d)}, device_id_type=MESH)
    pl.semaphore_signal(barrier, inc=1, device_id={"ctx": sibling}, device_id_type=MESH)
    for d in range(1, n_page):
        pl.semaphore_signal(
            barrier, inc=1, device_id={"page": (page + d) % n_page}, device_id_type=MESH
        )

    def slot(buf, owner):
        return buf.at[pl.ds(owner * spans, spans)]

    fetch(k_ref, slot(kbuf, me), 0)
    fetch(v_ref, slot(vbuf, me), 1)
    fetch(table_in, table_ref, 2)
    fetch(slots_in, slots_ref, 3)
    fetch(q_in, q_ref, 4)
    pl.semaphore_wait(barrier, chips + n_page - 1)

    def remote(src, buf, owner, index, j, target):
        return pltpu.make_async_remote_copy(
            src_ref=src,
            dst_ref=slot(buf, owner),
            send_sem=send.at[index, j],
            recv_sem=recv.at[index, j],
            device_id={"ctx": target},
            device_id_type=MESH,
        )

    pairs = ((k_ref, kbuf), (v_ref, vbuf))
    started = []
    for d in range(1, chips):
        for j, (src, buf) in enumerate(pairs):
            copy = remote(src, buf, me, d, j, ahead(d))
            copy.start()
            started.append(copy)
    for j, (src, buf) in enumerate(pairs):
        copy = remote(src, buf, me, 0, j, sibling)
        copy.start()
        started.append(copy)

    rows_at = lax.broadcasted_iota(jnp.int32, (SPAN, SPAN), 0)
    cols_at = lax.broadcasted_iota(jnp.int32, (SPAN, SPAN), 1)
    eye = jnp.where(rows_at == cols_at, 1.0, 0.0).astype(jnp.bfloat16)
    vone[:, DH:] = jnp.ones((wide, DH), jnp.bfloat16)

    def chunk(d, first):
        owner = (chip + chips - d) % chips
        begin = owner * 2 * spans
        for t in range(2 * spans):
            place = pl.ds(t * SPAN, SPAN)
            piece = kbuf[begin + t]
            vone[place, :DH] = vbuf[begin + t]
            for i in range(spans):
                gap = (table_ref[me * spans + i] - table_ref[begin + t]) * SPAN
                kmask[i, place, :DH] = piece
                kmask[i, place, DH:] = jnp.where(rows_at - cols_at > gap, HIDE, 0.0).astype(
                    jnp.bfloat16
                )

        def attend_group(g):
            for i in range(spans):
                lines = pl.ds(i * SPAN, SPAN)
                query = jnp.concatenate(
                    [
                        jnp.concatenate(
                            [
                                q_ref[lines, pl.ds(pl.multiple_of((g * per + h) * DH, DH), DH)],
                                eye,
                            ],
                            axis=1,
                        )
                        for h in range(per)
                    ],
                    axis=0,
                )
                score = lax.dot_general(
                    query, kmask[i], (((1,), (1,)), ((), ())), preferred_element_type=jnp.float32
                )
                high = jnp.broadcast_to(jnp.max(score, axis=1, keepdims=True), (size, DH))
                if not first:
                    old = top[g, i]
                    high = jnp.maximum(high, old)
                weight = jnp.concatenate(
                    [
                        jnp.exp2((score[:, t * SPAN : (t + 1) * SPAN] - high) * rate).astype(
                            jnp.bfloat16
                        )
                        for t in range(2 * spans)
                    ],
                    axis=1,
                )
                update = jnp.dot(weight, vone[...], preferred_element_type=jnp.float32)
                top[g, i] = high
                if first:
                    acc[g, i] = update
                else:
                    factor = jnp.exp2((old - high) * rate)
                    acc[g, i, :, :DH] = acc[g, i, :, :DH] * factor + update[:, :DH]
                    acc[g, i, :, DH:] = acc[g, i, :, DH:] * factor + update[:, DH:]

        return lambda: pl.loop(0, groups)(attend_group)

    for copy in local:
        copy.wait()
    for j, (src, buf) in enumerate(pairs):
        remote(src, buf, sibling, 0, j, sibling).wait_recv()
    chunk(0, True)()

    for d in range(1, chips):
        for j, (src, buf) in enumerate(pairs):
            origin = behind(d, core)
            remote(src, buf, origin, d, j, sibling).wait_recv()
            copy = remote(slot(buf, origin), buf, origin, chips - 1 + d, j, sibling)
            copy.start()
            started.append(copy)
    for d in range(1, chips):
        for j, (src, buf) in enumerate(pairs):
            remote(src, buf, behind(d, 1 - core), chips - 1 + d, j, sibling).wait_recv()

    for s in range(spans):
        wanted = jnp.int32(0)
        for p in range(slots_ref.shape[0]):
            wanted = jnp.where(slots_ref[p] == me * spans + s, p, wanted)
        for j, buf in enumerate((kbuf, vbuf)):
            raw = buf[wanted].astype(jnp.float32)
            level = jnp.max(jnp.max(jnp.abs(raw), axis=0, keepdims=True), axis=1, keepdims=True)
            level = level + 1e-06
            cache_ref[page, s, j] = (raw / level).astype(jnp.bfloat16)
            scales_ref[page, s, j] = jnp.broadcast_to(level, (8, DH))

    def pages(index, target):
        return [
            pltpu.make_async_remote_copy(
                src_ref=ref.at[page],
                dst_ref=ref.at[page],
                send_sem=page_send.at[index, j],
                recv_sem=page_recv.at[index, j],
                device_id={"page": target},
                device_id_type=MESH,
            )
            for j, ref in enumerate((cache_ref, scales_ref))
        ]

    def arrived(index):
        origin = (page + n_page - index) % n_page
        for j, ref in enumerate((cache_ref, scales_ref)):
            pltpu.make_async_remote_copy(
                src_ref=ref.at[origin],
                dst_ref=ref.at[origin],
                send_sem=page_send.at[index, j],
                recv_sem=page_recv.at[index, j],
                device_id={"page": (page + index) % n_page},
                device_id_type=MESH,
            ).wait_recv()

    for d in range(1, chips):
        attend = chunk(d, False)
        if d == 1:
            for index in range(1, n_page):
                for copy in pages(index, (page + index) % n_page):
                    copy.start()
                    started.append(copy)
        attend()

    @pl.loop(0, groups)
    def _(g):
        for i in range(spans):
            for h in range(per):
                lines = pl.ds(h * SPAN, SPAN)
                out_ref[
                    pl.ds(i * SPAN, SPAN), pl.ds(pl.multiple_of((g * per + h) * DH, DH), DH)
                ] = (acc[g, i, lines, :DH] / acc[g, i, lines, DH:]).astype(jnp.bfloat16)

    for index in range(1, n_page):
        arrived(index)
    for copy in started:
        copy.wait_send()


def on_device(n, n_page, queries, keys, values, span_table, page_slots):
    rows = queries.shape[0]
    heads = queries.shape[1] // DH
    spans = rows // SPAN
    per = math.gcd(heads, 4)
    groups = heads // per
    chips = n // 2
    wide = 2 * rows
    vmem = pl.BlockSpec(memory_space=pltpu.VMEM)
    hbm = pl.BlockSpec(memory_space=pltpu.HBM)
    attended, cache, scales = pl.pallas_call(
        functools.partial(kernel, n, n_page, heads),
        out_shape=(
            jax.ShapeDtypeStruct((rows, heads * DH), jnp.bfloat16),
            jax.ShapeDtypeStruct((n_page, spans, 2, PAGE, DH), jnp.bfloat16),
            jax.ShapeDtypeStruct((n_page, spans, 2, 8, DH), jnp.float32),
        ),
        in_specs=[hbm] * 5,
        out_specs=(vmem, vmem, vmem),
        scratch_shapes=[
            pltpu.SMEM(span_table.shape, jnp.int32),
            pltpu.SMEM(page_slots.shape, jnp.int32),
            pltpu.VMEM(queries.shape, jnp.bfloat16),
            pltpu.VMEM((n * spans, SPAN, DH), jnp.bfloat16),
            pltpu.VMEM((n * spans, SPAN, DH), jnp.bfloat16),
            pltpu.VMEM((spans, wide, 2 * DH), jnp.bfloat16),
            pltpu.VMEM((wide, 2 * DH), jnp.bfloat16),
            pltpu.VMEM((groups, spans, per * SPAN, 2 * DH), jnp.float32),
            pltpu.VMEM((groups, spans, per * SPAN, DH), jnp.float32),
            pltpu.SemaphoreType.DMA((n, 2)),
            pltpu.SemaphoreType.DMA((n, 2)),
            pltpu.SemaphoreType.DMA((5,)),
            pltpu.SemaphoreType.DMA((n_page, 2)),
            pltpu.SemaphoreType.DMA((n_page, 2)),
        ],
        compiler_params=pltpu.CompilerParams(
            collective_id=0, has_side_effects=True, vmem_limit_bytes=67043328
        ),
    )(
        span_table,
        page_slots,
        queries,
        keys.reshape(spans, SPAN, DH),
        values.reshape(spans, SPAN, DH),
    )
    cache = cache.transpose(1, 0, 2, 3, 4)
    scales = scales[:, :, :, 0, 0].transpose(1, 0, 2)
    return attended, cache, scales


def solution(mesh):
    placed = (P("ctx", "page"), P("ctx", "page"), P("ctx", "page"), P(), P())
    return jax.shard_map(
        functools.partial(on_device, mesh.shape["ctx"], mesh.shape["page"]),
        mesh=mesh,
        in_specs=placed,
        out_specs=(P("ctx", "page"), P("ctx", None, None, None, None), P("ctx", None, None)),
        check_vma=False,
    )
```

```python
import functools
import math

import jax
import jax.numpy as jnp
from jax import lax
from jax.experimental import pallas as pl
from jax.experimental.pallas import tpu as pltpu
from jax.sharding import PartitionSpec as P

DH = 128
PAGE = 128
SPAN = 128
HIDE = -1e30
MESH = pl.DeviceIdType.MESH


def kernel(
    n, n_page, heads, table_in, slots_in, q_in, k_ref, v_ref,
    out_ref, cache_ref, scales_ref,
    table_ref, slots_ref, q_ref,
    kbuf, vbuf, kmask, vone, acc, top, send, recv, own_sem, page_send, page_recv,
    level_send, level_recv,
):
    chips = n // 2
    spans = k_ref.shape[0]
    wide = 2 * spans * SPAN
    per = math.gcd(heads, 4)
    groups = heads // per
    size = per * SPAN
    me = lax.axis_index("ctx")
    page = lax.axis_index("page")
    chip = me // 2
    core = me % 2
    sibling = 2 * chip + 1 - core
    rate = DH ** (-0.5) * math.log2(math.e)

    def partner(d):
        other, bit = 0, 1
        while bit < chips:
            other = other + (chip // bit + d // bit) % 2 * bit
            bit *= 2
        return other

    def peer(d, c):
        return 2 * partner(d) + c

    local = []

    def fetch(src, dst, j):
        copy = pltpu.make_async_copy(src, dst, own_sem.at[j])
        copy.start()
        local.append(copy)

    barrier = pltpu.get_barrier_semaphore()
    for d in range(1, chips):
        pl.semaphore_signal(barrier, inc=1, device_id={"ctx": peer(d, core)}, device_id_type=MESH)
    pl.semaphore_signal(barrier, inc=1, device_id={"ctx": sibling}, device_id_type=MESH)
    for d in range(1, n_page):
        pl.semaphore_signal(
            barrier, inc=1, device_id={"page": (page + d) % n_page}, device_id_type=MESH
        )

    def slot(buf, owner):
        return buf.at[pl.ds(owner * spans, spans)]

    fetch(k_ref, slot(kbuf, me), 0)
    fetch(v_ref, slot(vbuf, me), 1)
    fetch(table_in, table_ref, 2)
    fetch(slots_in, slots_ref, 3)
    fetch(q_in, q_ref, 4)
    pl.semaphore_wait(barrier, chips + n_page - 1)

    def remote(src, buf, owner, index, j, target):
        return pltpu.make_async_remote_copy(
            src_ref=src,
            dst_ref=slot(buf, owner),
            send_sem=send.at[index, j],
            recv_sem=recv.at[index, j],
            device_id={"ctx": target},
            device_id_type=MESH,
        )

    pairs = ((k_ref, kbuf), (v_ref, vbuf))
    started = []
    for d in range(1, chips):
        for j, (src, buf) in enumerate(pairs):
            copy = remote(src, buf, me, d, j, peer(d, core))
            copy.start()
            started.append(copy)
    for j, (src, buf) in enumerate(pairs):
        copy = remote(src, buf, me, 0, j, sibling)
        copy.start()
        started.append(copy)

    rows_at = lax.broadcasted_iota(jnp.int32, (SPAN, SPAN), 0)
    cols_at = lax.broadcasted_iota(jnp.int32, (SPAN, SPAN), 1)
    eye = jnp.where(rows_at == cols_at, 1.0, 0.0).astype(jnp.bfloat16)
    vone[:, DH:] = jnp.ones((wide, DH), jnp.bfloat16)

    def chunk(d, first):
        owner = partner(d)
        begin = owner * 2 * spans
        for t in range(2 * spans):
            place = pl.ds(t * SPAN, SPAN)
            piece = kbuf[begin + t]
            vone[place, :DH] = vbuf[begin + t]
            for i in range(spans):
                gap = (table_ref[me * spans + i] - table_ref[begin + t]) * SPAN
                kmask[i, place, :DH] = piece
                kmask[i, place, DH:] = jnp.where(rows_at - cols_at > gap, HIDE, 0.0).astype(
                    jnp.bfloat16
                )

        def attend_group(g):
            for i in range(spans):
                lines = pl.ds(i * SPAN, SPAN)
                query = jnp.concatenate(
                    [
                        jnp.concatenate(
                            [
                                q_ref[lines, pl.ds(pl.multiple_of((g * per + h) * DH, DH), DH)],
                                eye,
                            ],
                            axis=1,
                        )
                        for h in range(per)
                    ],
                    axis=0,
                )
                score = lax.dot_general(
                    query, kmask[i], (((1,), (1,)), ((), ())), preferred_element_type=jnp.float32
                )
                high = jnp.broadcast_to(jnp.max(score, axis=1, keepdims=True), (size, DH))
                if not first:
                    old = top[g, i]
                    high = jnp.maximum(high, old)
                weight = jnp.concatenate(
                    [
                        jnp.exp2((score[:, t * SPAN : (t + 1) * SPAN] - high) * rate).astype(
                            jnp.bfloat16
                        )
                        for t in range(2 * spans)
                    ],
                    axis=1,
                )
                update = jnp.dot(weight, vone[...], preferred_element_type=jnp.float32)
                top[g, i] = high
                if first:
                    acc[g, i] = update
                else:
                    factor = jnp.exp2((old - high) * rate)
                    acc[g, i, :, :DH] = acc[g, i, :, :DH] * factor + update[:, :DH]
                    acc[g, i, :, DH:] = acc[g, i, :, DH:] * factor + update[:, DH:]

        return lambda: pl.loop(0, groups)(attend_group)

    for copy in local:
        copy.wait()
    for j, (src, buf) in enumerate(pairs):
        remote(src, buf, sibling, 0, j, sibling).wait_recv()
    chunk(0, True)()

    def relay(d):
        for j, (src, buf) in enumerate(pairs):
            origin = peer(d, core)
            remote(src, buf, origin, d, j, sibling).wait_recv()
            copy = remote(slot(buf, origin), buf, origin, chips - 1 + d, j, sibling)
            copy.start()
            started.append(copy)

    def landed(d):
        for j, (src, buf) in enumerate(pairs):
            remote(src, buf, peer(d, 1 - core), chips - 1 + d, j, sibling).wait_recv()

    half = chips // 2
    for d in range(1, half + 1):
        relay(d)
    for d in range(1, half):
        landed(d)
        chunk(d, False)()
    for d in range(half + 1, chips):
        relay(d)
    for d in range(half, chips):
        landed(d)

    for s in range(spans):
        wanted = jnp.int32(0)
        for p in range(slots_ref.shape[0]):
            wanted = jnp.where(slots_ref[p] == me * spans + s, p, wanted)
        for j, buf in enumerate((kbuf, vbuf)):
            raw = buf[wanted].astype(jnp.float32)
            level = jnp.max(jnp.max(jnp.abs(raw), axis=0, keepdims=True), axis=1, keepdims=True)
            level = level + 1e-06
            cache_ref[page, j, s] = (raw / level).astype(jnp.bfloat16)
            scales_ref[page, s, j] = jnp.broadcast_to(level, (8, DH))

    reach = n_page // 2

    def hop(k, j, way):
        origin = (page + n_page - way * (k - 1)) % n_page
        return pltpu.make_async_remote_copy(
            src_ref=cache_ref.at[origin, j],
            dst_ref=cache_ref.at[origin, j],
            send_sem=page_send.at[k, j, (way + 1) // 2],
            recv_sem=page_recv.at[k, j, (way + 1) // 2],
            device_id={"page": (page + n_page + way) % n_page},
            device_id_type=MESH,
        )

    def coming(k, j, way):
        origin = (page + n_page - way * k) % n_page
        return pltpu.make_async_remote_copy(
            src_ref=cache_ref.at[origin, j],
            dst_ref=cache_ref.at[origin, j],
            send_sem=page_send.at[k, j, (way + 1) // 2],
            recv_sem=page_recv.at[k, j, (way + 1) // 2],
            device_id={"page": (page + n_page + way) % n_page},
            device_id_type=MESH,
        )

    def used(k):
        both = [(0, 1), (1, -1), (1, 1), (0, -1)]
        return both[:2] if 2 * k == n_page else both

    def send_hop(k):
        for j, way in used(k):
            if k > 1:
                coming(k - 1, j, way).wait_recv()
            copy = hop(k, j, way)
            copy.start()
            started.append(copy)

    def levels(index, origin):
        return pltpu.make_async_remote_copy(
            src_ref=scales_ref.at[origin],
            dst_ref=scales_ref.at[origin],
            send_sem=level_send.at[index],
            recv_sem=level_recv.at[index],
            device_id={"page": (page + index) % n_page},
            device_id_type=MESH,
        )

    for d in range(half, chips):
        attend = chunk(d, False)
        if d == half:
            send_hop(1)
            for index in range(1, n_page):
                copy = levels(index, page)
                copy.start()
                started.append(copy)
        attend()
        if d == half:
            for k in range(2, reach + 1):
                send_hop(k)

    @pl.loop(0, groups)
    def _(g):
        for i in range(spans):
            for h in range(per):
                lines = pl.ds(h * SPAN, SPAN)
                out_ref[
                    pl.ds(i * SPAN, SPAN), pl.ds(pl.multiple_of((g * per + h) * DH, DH), DH)
                ] = (acc[g, i, lines, :DH] / acc[g, i, lines, DH:]).astype(jnp.bfloat16)

    for index in range(1, n_page):
        levels(index, (page + n_page - index) % n_page).wait_recv()
    for k in range(1, reach + 1):
        passed = used(k + 1) if k < reach else []
        for j, way in used(k):
            if (j, way) not in passed:
                coming(k, j, way).wait_recv()
    for copy in started:
        copy.wait_send()


def on_device(n, n_page, queries, keys, values, span_table, page_slots):
    rows = queries.shape[0]
    heads = queries.shape[1] // DH
    spans = rows // SPAN
    per = math.gcd(heads, 4)
    groups = heads // per
    chips = n // 2
    wide = 2 * rows
    vmem = pl.BlockSpec(memory_space=pltpu.VMEM)
    hbm = pl.BlockSpec(memory_space=pltpu.HBM)
    attended, cache, scales = pl.pallas_call(
        functools.partial(kernel, n, n_page, heads),
        out_shape=(
            jax.ShapeDtypeStruct((rows, heads * DH), jnp.bfloat16),
            jax.ShapeDtypeStruct((n_page, 2, spans, PAGE, DH), jnp.bfloat16),
            jax.ShapeDtypeStruct((n_page, spans, 2, 8, DH), jnp.float32),
        ),
        in_specs=[hbm] * 5,
        out_specs=(vmem, vmem, vmem),
        scratch_shapes=[
            pltpu.SMEM(span_table.shape, jnp.int32),
            pltpu.SMEM(page_slots.shape, jnp.int32),
            pltpu.VMEM(queries.shape, jnp.bfloat16),
            pltpu.VMEM((n * spans, SPAN, DH), jnp.bfloat16),
            pltpu.VMEM((n * spans, SPAN, DH), jnp.bfloat16),
            pltpu.VMEM((spans, wide, 2 * DH), jnp.bfloat16),
            pltpu.VMEM((wide, 2 * DH), jnp.bfloat16),
            pltpu.VMEM((groups, spans, per * SPAN, 2 * DH), jnp.float32),
            pltpu.VMEM((groups, spans, per * SPAN, DH), jnp.float32),
            pltpu.SemaphoreType.DMA((n, 2)),
            pltpu.SemaphoreType.DMA((n, 2)),
            pltpu.SemaphoreType.DMA((5,)),
            pltpu.SemaphoreType.DMA((n_page // 2 + 1, 2, 2)),
            pltpu.SemaphoreType.DMA((n_page // 2 + 1, 2, 2)),
            pltpu.SemaphoreType.DMA((n_page,)),
            pltpu.SemaphoreType.DMA((n_page,)),
        ],
        compiler_params=pltpu.CompilerParams(
            collective_id=0, has_side_effects=True, vmem_limit_bytes=67043328
        ),
    )(
        span_table,
        page_slots,
        queries,
        keys.reshape(spans, SPAN, DH),
        values.reshape(spans, SPAN, DH),
    )
    cache = cache.transpose(2, 0, 1, 3, 4)
    scales = scales[:, :, :, 0, 0].transpose(1, 0, 2)
    return attended, cache, scales


def solution(mesh):
    placed = (P("ctx", "page"), P("ctx", "page"), P("ctx", "page"), P(), P())
    return jax.shard_map(
        functools.partial(on_device, mesh.shape["ctx"], mesh.shape["page"]),
        mesh=mesh,
        in_specs=placed,
        out_specs=(P("ctx", "page"), P("ctx", None, None, None, None), P("ctx", None, None)),
        check_vma=False,
    )
```
